32 devices in a mesh: section: 2 (over core), rows: 4 (over z), cols: 4 (over y, x).
Axes of the slice: x: 2, y: 2, z: 4, core: 2. Of those that a mesh axis runs over, the one named last changes fastest.
Arguments:
- images: bfloat16 [8224, 1280], P('rows', 'cols'), may hold values from -6 to 6
- cotangent: bfloat16 [8224, 1280], P('rows', 'cols'), may hold values from -6 to 6
- live_images: int32 [4, 2], P('rows'), may hold values from 1 to 4, as said below
- attn_norm_gain: bfloat16 [2, 1280], P('section', 'cols'), may hold values from 0.5 to 1.5
- attn_norm_bias: bfloat16 [2, 1280], P('section', 'cols'), may hold values from -3 to 3
- qkv_weight: bfloat16 [2, 1280, 3, 1280], P('section', 'rows', None, 'cols'), may hold values from -0.15625 to 0.15625
- query_value_bias: bfloat16 [2, 2, 1280], P('section', None, 'cols'), may hold values from -3 to 3
- out_weight: bfloat16 [2, 1280, 1280], P('section', 'cols', 'rows'), may hold values from -1.25 to 1.25
- out_bias: bfloat16 [2, 1280], P('section', 'cols'), may hold values from -3 to 3
- mlp_norm_gain: bfloat16 [2, 1280], P('section', 'cols'), may hold values from 0.5 to 1.5
- mlp_norm_bias: bfloat16 [2, 1280], P('section', 'cols'), may hold values from -3 to 3
- up_weight: bfloat16 [2, 1280, 5120], P('section', 'rows', 'cols'), may hold values from -0.15625 to 0.15625
- up_bias: bfloat16 [2, 5120], P('section', 'cols'), may hold values from -3 to 3
- down_weight: bfloat16 [2, 5120, 1280], P('section', 'cols', 'rows'), may hold values from -0.078125 to 0.078125
- down_bias: bfloat16 [2, 1280], P('section', 'cols'), may hold values from -3 to 3
Outputs:
- section_outputs: bfloat16 [2, 8224, 1280], P('section', 'rows', 'cols')
- input_grads: bfloat16 [2, 8224, 1280], P('section', 'rows', 'cols')
- grad_attn_norm_gain: float32 [2, 1280], P('section', 'cols')
- grad_attn_norm_bias: float32 [2, 1280], P('section', 'cols')
- grad_qkv_weight: float32 [2, 1280, 3, 1280], P('section', 'rows', None, 'cols')
- grad_query_value_bias: float32 [2, 2, 1280], P('section', None, 'cols')
- grad_out_weight: float32 [2, 1280, 1280], P('section', 'cols', 'rows')
- grad_out_bias: float32 [2, 1280], P('section', 'cols')
- grad_mlp_norm_gain: float32 [2, 1280], P('section', 'cols')
- grad_mlp_norm_bias: float32 [2, 1280], P('section', 'cols')
- grad_up_weight: float32 [2, 1280, 5120], P('section', 'rows', 'cols')
- grad_up_bias: float32 [2, 5120], P('section', 'cols')
- grad_down_weight: float32 [2, 5120, 1280], P('section', 'cols', 'rows')
- grad_down_bias: float32 [2, 1280], P('section', 'cols')
The draws below stay inside these ranges and needn't reach their ends.
Inputs may be any that keep to these rules, and one draw needn't show every extreme that they name: `live_images`: each entry counts the live image slots of one micro-batch on one token block; in every micro-batch some token block holds 4.
All inputs are finite; a program needn't handle non-finite values.
Results may differ from the reference program's by a relative error of at most 0.017.
Values may be sent and summed in bfloat16 or wider, within the bound.
No kernel may reach another device: no remote copies, remote signals or barrier semaphores. Data moves between devices by JAX's collectives and lax.ppermute only.
A program may use at most 256 MiB of HBM per device.

```python
import jax
import jax.numpy as jnp
from jax import lax

D = 1280
HEADS = 16
HEAD_DIM = 80
FF = 5120
SEQ = 257
MICRO = 2
IMG_CAP = 4
SECTIONS = 2
ROW_BLOCKS = 4
TOKENS = 8224


def draw_live_images(key, part):
    counts = jax.random.randint(jax.random.fold_in(key, 11), (ROW_BLOCKS, MICRO), 1, IMG_CAP + 1)
    fullest = jax.random.randint(jax.random.fold_in(key, 12), (MICRO,), 0, ROW_BLOCKS)
    chosen = jnp.arange(ROW_BLOCKS, dtype=jnp.int32)[:, None] == fullest[None, :]
    return jnp.where(chosen, IMG_CAP, counts).astype(jnp.int32)


def shard_levels(rng, dims, split, least, high):
    level, own = 1.0, jax.random.fold_in(rng, 6)
    for axis_at, shards_of in split:
        draws = jnp.exp(jax.random.uniform(jax.random.fold_in(own, axis_at), (shards_of,), jnp.float32, least / len(split), high / len(split)))
        level = level * jnp.repeat(draws, dims[axis_at] // shards_of).reshape([-1 if axis == axis_at else 1 for axis in range(len(dims))])
    return level


def scatter_about(own_key, shape, deviation, most, split=(), kind=jnp.bfloat16):
    loudness = shard_levels(own_key, shape, split, -0.22, 0.18) if split else 1.0
    values = jax.random.normal(own_key, shape, jnp.float32) * deviation * loudness
    return jnp.minimum(jnp.maximum(values, -most), most).astype(kind)


def setup_inputs(seed: int = 0) -> dict:
    key_list = jax.random.split(jax.random.key(seed), 16)
    return {
        "images": scatter_about(key_list[0], (TOKENS, D), 1.0, 6.0, ((0, 4), (1, 4))),
        "cotangent": scatter_about(key_list[1], (TOKENS, D), 1.0, 6.0, ((0, 4), (1, 4))),
        "live_images": draw_live_images(jax.random.fold_in(key_list[15], 71), 0),
        "attn_norm_gain": jnp.clip(1.0 + 0.1 * jax.random.normal(key_list[3], (SECTIONS, D), jnp.float32), 0.5, 1.5).astype(jnp.bfloat16),
        "attn_norm_bias": scatter_about(key_list[4], (SECTIONS, D), 0.5, 3.0, ((0, 2), (1, 4))),
        "qkv_weight": scatter_about(key_list[5], (SECTIONS, D, 3, D), D ** -0.5, 0.15625, ((0, 2), (1, 4), (3, 4))),
        "query_value_bias": scatter_about(key_list[6], (SECTIONS, 2, D), 0.5, 3.0, ((0, 2), (2, 4))),
        "out_weight": scatter_about(key_list[7], (SECTIONS, D, D), (D // 64) ** -0.5, 1.25, ((0, 2), (1, 4), (2, 4))),
        "out_bias": scatter_about(key_list[8], (SECTIONS, D), 0.5, 3.0, ((0, 2), (1, 4))),
        "mlp_norm_gain": jnp.clip(1.0 + 0.1 * jax.random.normal(key_list[9], (SECTIONS, D), jnp.float32), 0.5, 1.5).astype(jnp.bfloat16),
        "mlp_norm_bias": scatter_about(key_list[10], (SECTIONS, D), 0.5, 3.0, ((0, 2), (1, 4))),
        "up_weight": scatter_about(key_list[11], (SECTIONS, D, FF), D ** -0.5, 0.15625, ((0, 2), (1, 4), (2, 4))),
        "up_bias": scatter_about(key_list[12], (SECTIONS, FF), 0.5, 3.0, ((0, 2), (1, 4))),
        "down_weight": scatter_about(key_list[13], (SECTIONS, FF, D), FF ** -0.5, 0.078125, ((0, 2), (1, 4), (2, 4))),
        "down_bias": scatter_about(key_list[14], (SECTIONS, D), 0.5, 3.0, ((0, 2), (1, 4))),
    }


epsilon = 1e-06
highest = lax.Precision.HIGHEST

@jax.custom_vjp
def low(v):
    return lax.optimization_barrier(v.astype(jnp.bfloat16)).astype(jnp.float32)

@jax.custom_vjp
def low_back(v):
    return v

def low_keep(v):
    return (low(v), None)

def low_pass(kept, grad):
    return (grad,)

def back_keep(v):
    return (v, None)

def back_low(kept, grad):
    return (low(grad),)
low.defvjp(low_keep, low_pass)
low_back.defvjp(back_keep, back_low)

def norm_rows(values, gain, shift):
    centre = lax.optimization_barrier(jnp.mean(values, axis=-1, keepdims=True))
    centred = values - centre
    spread = lax.optimization_barrier(jnp.mean(centred * centred, axis=-1, keepdims=True))
    return centred * lax.rsqrt(spread + epsilon) * gain + shift

def encoder_layer(values, params):
    norm1_gain, norm1_bias, qkv_full, qv_pair, out_full, attn_bias, norm2_gain, norm2_bias, up_full, hidden_bias, down_full, output_bias = params
    normed = low(norm_rows(values, norm1_gain, norm1_bias))
    projected = jnp.einsum('td,dcf->tcf', normed, qkv_full, precision=highest)
    bias_three = jnp.stack([qv_pair[0], jnp.zeros_like(qv_pair[0]), qv_pair[1]])
    projected = low_back(low(projected + bias_three))
    image_count = projected.shape[0] // SEQ
    per_head = projected.reshape(image_count, SEQ, 3, HEADS, HEAD_DIM)
    queries = per_head[:, :, 0]
    key_heads = per_head[:, :, 1]
    value_heads = per_head[:, :, 2]
    scores = low_back(jnp.einsum('isnh,itnh->inst', queries, key_heads, precision=highest) * HEAD_DIM ** (-0.5))
    softened = low(jax.nn.softmax(scores, axis=-1))
    head_out = jnp.einsum('inst,itnh->isnh', softened, value_heads, precision=highest).reshape(-1, D)
    head_out = low_back(low(head_out))
    attn_out = low_back(jnp.dot(head_out, out_full, precision=highest) + attn_bias)
    residual = values + attn_out
    normed_two = low(norm_rows(residual, norm2_gain, norm2_bias))
    pre_act = low_back(jnp.dot(normed_two, up_full, precision=highest) + hidden_bias)
    activated = low(jax.nn.gelu(pre_act, approximate=False))
    down_out = low_back(jnp.dot(activated, down_full, precision=highest) + output_bias)
    return low(residual + down_out)

def reference(images, cotangent, live_images, attn_norm_gain, attn_norm_bias, qkv_weight, query_value_bias, out_weight, out_bias, mlp_norm_gain, mlp_norm_bias, up_weight, up_bias, down_weight, down_bias):
    slot_index = jnp.arange(IMG_CAP, dtype=jnp.int32)
    live = (slot_index[None, :] < live_images.reshape(-1)[:, None]).astype(jnp.float32)
    live_mask = jnp.repeat(live.reshape(-1), SEQ)[:, None]
    params = tuple((member.astype(jnp.float32) for member in (attn_norm_gain, attn_norm_bias, qkv_weight, query_value_bias, out_weight, out_bias, mlp_norm_gain, mlp_norm_bias, up_weight, up_bias, down_weight, down_bias)))

    def masked_layer(values, weights):
        return encoder_layer(values, weights) * live_mask
    current = images.astype(jnp.float32)
    pullbacks = []
    section_list = []
    for section_number in range(SECTIONS):
        layer_params = tuple((member[section_number] for member in params))
        produced, pullback = jax.vjp(masked_layer, current, layer_params)
        pullbacks.append(pullback)
        section_list.append(produced.astype(jnp.bfloat16))
        current = produced
    upstream = cotangent.astype(jnp.float32) * live_mask
    input_list = [None] * SECTIONS
    param_list = [None] * SECTIONS
    for section_number in reversed(range(SECTIONS)):
        grad_values, grad_weights = pullbacks[section_number](upstream)
        rounded = grad_values.astype(jnp.bfloat16)
        input_list[section_number] = rounded
        param_list[section_number] = grad_weights
        upstream = rounded.astype(jnp.float32)
    stacked = [jnp.stack([param_list[number][which] for number in range(SECTIONS)]) for which in range(12)]
    return (jnp.stack(section_list), jnp.stack(input_list), stacked[0], stacked[1], stacked[2], stacked[3], stacked[4], stacked[5], stacked[6], stacked[7], stacked[8], stacked[9], stacked[10], stacked[11])
```

```python
import functools
import math

import jax
import jax.numpy as jnp
from jax import lax
from jax.experimental import pallas as pl
from jax.experimental.pallas import tpu as pltpu
from jax.sharding import PartitionSpec as P


HEAD_DIM = 80
SEQ = 257
LANES = 128
IMG_CAP = 4
EPSILON = 1e-06
SCALE = HEAD_DIM ** (-0.5)
CHUNK = 256


f32 = jnp.float32
bf16 = jnp.bfloat16

ROWS, COLS, CORE = "rows", "cols", "section"
ATTN, MLP, ATTN_GRAD, MLP_GRAD, _ = "ambno"

GAIN1, SHIFT1, OUT_BIAS, GAIN2, SHIFT2, DOWN_BIAS, QUERY, VALUE, HIDDEN = range(9)
FEATURES, VECTORS = 6, 12

TAIL = (
    0.08459480851888657,
    0.08534596860408783,
    0.07424121350049973,
    0.10721813142299652,
    -0.046815600246191025,
    0.2731974720954895,
    -0.25561317801475525,
    0.24254821240901947,
    -0.06471703946590424,
)


def flip(value, on_first, on_second):
    count = lax.axis_size(COLS)
    pairs = []
    for core, bits in ((0, on_first), (1, on_second)):
        pairs += [(core * count + k, core * count + (k ^ bits)) for k in range(count)]
    return lax.ppermute(value, (CORE, COLS), pairs)


def near(value):
    return flip(value, 1, 2)


def side(value):
    return flip(value, 2, 1)


def hops(parts):
    return [parts[0]] + [flip(parts[r], r, r) for r in range(1, IMG_CAP)]


def other_core(value):
    count = lax.axis_size(CORE)
    return lax.ppermute(value, CORE, [(k, count - 1 - k) for k in range(count)])


def spread(value):
    first = near(value)
    second = side(value)
    third = side(first)
    return [value, first, second, third]


def fold(terms, stage):
    own, first, second, third = terms
    passing = side(third)
    passed, token = run(
        add_kernel, [first, passing], [(first.shape, bf16), ((8, LANES), f32)], first.size
    )
    aside = side(second)
    passed = near(passed)
    if not stage.startswith((ATTN, MLP)):
        return own, aside, passed
    token = other_core(token)
    return own, aside, passed, token


def add_kernel(first_ref, second_ref, out_ref, token_ref):
    out_ref[...] = (first_ref[...].astype(f32) + second_ref[...].astype(f32)).astype(bf16)
    token_ref[...] = jnp.zeros_like(token_ref)


def dot(a, b, left, right):
    return lax.dot_general(a, b, (((left,), (right,)), ((), ())), preferred_element_type=f32)


def run(kernel, arrays, outs, flops, exps=0, scratch=(), room=12):
    specs = []
    for a in arrays:
        space = pltpu.SMEM if a.dtype == jnp.int32 else pltpu.VMEM
        specs.append(pl.BlockSpec(memory_space=space))
    moved = sum(a.size * a.dtype.itemsize for a in arrays)
    moved += sum(math.prod(s) * jnp.dtype(t).itemsize for s, t in outs)
    return pl.pallas_call(
        kernel,
        out_shape=[jax.ShapeDtypeStruct(s, t) for s, t in outs],
        in_specs=specs,
        out_specs=[pl.BlockSpec(memory_space=pltpu.VMEM) for _ in outs],
        scratch_shapes=list(scratch),
        cost_estimate=pl.CostEstimate(flops=flops, bytes_accessed=moved, transcendentals=exps),
        compiler_params=pltpu.CompilerParams(vmem_limit_bytes=room * 2**20),
    )(*arrays)


def each_place(spot_ref, write, cores=True):
    for core in range(2 if cores else 1):
        for me in range(IMG_CAP):
            here = spot_ref[0, 1] == me
            if cores:
                here = here & (spot_ref[0, 0] == core)
            pl.when(here)(functools.partial(write, core, me))


def pick_kernel(spot_ref, images_ref, *out_refs):
    def write(core, me):
        for r, out_ref in enumerate(out_refs):
            at = (core * IMG_CAP + (me ^ r)) * SEQ
            out_ref[...] = images_ref[at : at + SEQ, :]

    each_place(spot_ref, write)


def join_blocks(me, blocks, out_ref):
    width = blocks[0].shape[1]
    for r in range(IMG_CAP):
        out_ref[:, (me ^ r) * width : ((me ^ r) + 1) * width] = blocks[r][...]


def join_kernel(spot_ref, *refs):
    blocks, small = refs[:IMG_CAP], refs[IMG_CAP : 2 * IMG_CAP]
    x_ref, vector_ref, out_ref = refs[2 * IMG_CAP :]

    def write(core, me):
        join_blocks(me, blocks, x_ref)
        width = blocks[0].shape[1]
        for r in range(IMG_CAP):
            span = slice((me ^ r) * width, ((me ^ r) + 1) * width)
            for layer in range(2):
                at, to = layer * VECTORS, layer * FEATURES
                vector_ref[to : to + FEATURES, span] = small[r][at : at + FEATURES, :]

    each_place(spot_ref, write, cores=False)
    standard, _ = standardize(x_ref[...].astype(f32))
    out_ref[...] = (standard * row(vector_ref, 0, GAIN1) + row(vector_ref, 0, SHIFT1)).astype(bf16)


def join_target_kernel(spot_ref, *refs):
    out_ref = refs[IMG_CAP]

    def write(core, me):
        join_blocks(me, refs[:IMG_CAP], out_ref)

    each_place(spot_ref, write, cores=False)
    target = out_ref[...]
    out_ref[...] = jnp.where(spot_ref[0, 2] > 0, target, jnp.zeros_like(target))


def line_kernel(rows, spot_ref, *refs):
    mine, below, above, out_ref = refs[0], refs[1:rows], refs[rows : 2 * rows - 1], refs[-1]
    size = mine.shape[0]
    for z in range(rows):

        def write(z=z):
            for n in range(rows):
                block = mine if n == z else below[z - n - 1] if n < z else above[n - z - 1]
                out_ref[n * size : (n + 1) * size, :] = block[...]

        pl.when(spot_ref[0, 3] == z)(write)


def interleave_kernel(rows, spot_ref, mine_ref, got_ref, out_ref):
    half = mine_ref.shape[0] // rows
    for core in range(2):

        def write(core=core):
            low, high = (mine_ref, got_ref) if core == 0 else (got_ref, mine_ref)
            for z in range(rows):
                span = slice(z * half, (z + 1) * half)
                out_ref[2 * z * half : (2 * z + 1) * half, :] = low[span, :]
                out_ref[(2 * z + 1) * half : (2 * z + 2) * half, :] = high[span, :]

        pl.when(spot_ref[0, 0] == core)(write)


def line_gather(block, spot):
    rows = lax.axis_size(ROWS)
    below, above = [block], [block]
    for _ in range(rows - 1):
        below.append(lax.ppermute(below[-1], ROWS, [(k, k + 1) for k in range(rows - 1)]))
        above.append(lax.ppermute(above[-1], ROWS, [(k + 1, k) for k in range(rows - 1)]))
    half, width = block.shape
    (mine,) = run(
        functools.partial(line_kernel, rows),
        [spot, block, *below[1:], *above[1:]],
        [((rows * half, width), bf16)],
        1,
    )
    got = other_core(mine)
    (whole,) = run(
        functools.partial(interleave_kernel, rows),
        [spot, mine, got],
        [((2 * rows * half, width), bf16)],
        1,
    )
    return whole


def split_kernel(spot_ref, mine_ref, got_ref, *out_refs):
    width = out_refs[0].shape[2]

    def write(core, me):
        both = (mine_ref, got_ref) if core == 0 else (got_ref, mine_ref)
        for r, out_ref in enumerate(out_refs):
            span = slice((me ^ r) * width, ((me ^ r) + 1) * width)
            out_ref[0] = both[0][:, span]
            out_ref[1] = both[1][:, span]

    each_place(spot_ref, write)


def place_kernel(spot_ref, *refs):
    out_ref = refs[IMG_CAP]

    def write(core, me):
        for r in range(IMG_CAP):
            for micro in range(2):
                at = (micro * IMG_CAP + (me ^ r)) * SEQ
                out_ref[at : at + SEQ, :] = refs[r][micro]

    each_place(spot_ref, write, cores=False)


def row(ref, layer, n):
    return ref[layer * FEATURES + n : layer * FEATURES + n + 1, :]


def tile_start(width):
    return width // LANES * LANES


def head_spans(width, start):
    lead = width - tile_start(width)
    return [slice(lead + n * width + start, lead + n * width + start + HEAD_DIM) for n in range(3)]


def attention_kernel(layer, f_ref, w_ref, local_ref, part_ref, qkv_ref, head_ref, lse_ref):
    width = head_ref.shape[1]
    at = layer * VECTORS
    query, value = (local_ref[at + n : at + n + 1, :] for n in (QUERY, VALUE))
    start = tile_start(width)
    nothing = jnp.zeros((1, width - start), f32)
    bias = jnp.concatenate([nothing, query, jnp.zeros_like(query), value], axis=1)
    qkv = (dot(f_ref[...], w_ref[:, start:], 1, 0) + bias).astype(bf16)
    qkv_ref[...] = qkv
    mixed = []
    for start in range(0, width, HEAD_DIM):
        q, k, v = (qkv[:, span] for span in head_spans(width, start))
        scores = dot(q, k, 1, 1) * SCALE
        largest = jnp.max(scores, axis=1, keepdims=True)
        raised = jnp.exp(scores - largest)
        total = jnp.sum(raised, axis=1, keepdims=True)
        probs = (raised * (1.0 / total)).astype(bf16)
        mixed.append(dot(probs, v, 1, 0).astype(bf16))
        head = start // HEAD_DIM
        lse_ref[:, head : head + 1] = largest + jnp.log(total)
    heads = jnp.concatenate(mixed, axis=1)
    head_ref[...] = heads
    part_ref[...] = dot(heads, w_ref[:, :width], 1, 1).astype(bf16)


def attention_image(layer, feats, weight, local):
    model, width = weight.shape[0], local.shape[1]
    inner = 4 * width - tile_start(width)
    return run(
        functools.partial(attention_kernel, layer),
        [feats, weight, local],
        [((SEQ, model), bf16), ((SEQ, inner), bf16), ((SEQ, width), bf16), ((SEQ, 128), f32)],
        2 * SEQ * (model * (inner + width) + 2 * SEQ * width),
        width // HEAD_DIM * SEQ * SEQ,
    )


def add_sum(refs, span, value):
    total = jnp.broadcast_to(
        jnp.sum(value.astype(f32), axis=0, keepdims=True), (8, value.shape[1])
    )
    if len(refs) > 1:
        total = total + refs[0][:, span]
    refs[-1][:, span] = total


def attention_grad_kernel(g_ref, qkv_ref, lse_ref, w_ref, *refs):
    *before, part_ref, dqkv_ref, sum_ref = refs
    lead = w_ref.shape[1] - qkv_ref.shape[1]
    width = w_ref.shape[1] // 4
    grad_heads = dot(g_ref[...], w_ref[:, :width], 1, 0).astype(bf16)
    qkv = qkv_ref[...]
    grads = [[], [], []]
    for start in range(0, width, HEAD_DIM):
        q, k, v = (qkv[:, span] for span in head_spans(width, start))
        head = start // HEAD_DIM
        grad_out = grad_heads[:, start : start + HEAD_DIM]
        probs = jnp.exp(dot(q, k, 1, 1) * SCALE - lse_ref[:, head : head + 1])
        grad_probs = dot(grad_out, v, 1, 1)
        inner = jnp.sum(probs * grad_probs, axis=1, keepdims=True)
        grad_scores = (probs * (grad_probs - inner)).astype(bf16)
        grads[0].append((dot(grad_scores, k, 1, 0) * SCALE).astype(bf16))
        grads[1].append((dot(grad_scores, q, 0, 0) * SCALE).astype(bf16))
        grads[2].append(dot(probs.astype(bf16), grad_out, 0, 0).astype(bf16))
    blank = jnp.zeros((SEQ, width - lead), bf16)
    dqkv = jnp.concatenate([blank] + grads[0] + grads[1] + grads[2], axis=1)
    dqkv_ref[...] = dqkv
    part_ref[...] = dot(dqkv, w_ref[:, lead:], 1, 1).astype(bf16)
    add_sum([*before, sum_ref], slice(None), dqkv)


def attention_grad_image(grad, qkv, lse, weight, before):
    model, inner = weight.shape[0], qkv.shape[1]
    width = weight.shape[1] // 4
    return run(
        attention_grad_kernel,
        [grad, qkv, lse, weight, *before],
        [((SEQ, model), bf16), ((SEQ, inner), bf16), ((8, inner), f32)],
        2 * SEQ * (model * (inner + width) + 5 * SEQ * width),
        width // HEAD_DIM * SEQ * SEQ,
    )


def chunks(total):
    size = math.gcd(total, CHUNK)
    return [slice(s, s + size) for s in range(0, total, size)]


def mlp_kernel(layer, f_ref, w_ref, local_ref, part_ref, act_ref, slope_ref):
    hidden = act_ref.shape[1]
    at = layer * VECTORS + HIDDEN
    count = hidden // local_ref.shape[1]
    bias = jnp.concatenate([local_ref[at + n : at + n + 1, :] for n in range(count)], axis=1)
    for span in chunks(hidden):
        pre = dot(f_ref[...], w_ref[:, span], 1, 0) + bias[:, span]
        t = 1.0 / (1.0 + (0.3 * 0.5**0.5) * jnp.abs(pre))
        tail = TAIL[-1]
        for value in TAIL[-2::-1]:
            tail = tail * t + value
        bell = jnp.exp(-0.5 * pre * pre)
        tail = tail * t * bell
        phi = jnp.where(pre >= 0.0, 1.0 - tail, tail)
        act_ref[:, span] = (pre * phi).astype(bf16)
        slope_ref[:, span] = (phi + pre * bell * (1.0 / math.sqrt(2.0 * math.pi))).astype(bf16)
    active = act_ref[...]
    for span in chunks(part_ref.shape[1]):
        part_ref[:, span] = dot(active, w_ref[span, hidden:], 1, 1).astype(bf16)


def mlp_image(layer, feats, weight, local):
    model, hidden = weight.shape[0], weight.shape[1] // 2
    return run(
        functools.partial(mlp_kernel, layer),
        [feats, weight, local],
        [((SEQ, model), bf16), ((SEQ, hidden), bf16), ((SEQ, hidden), bf16)],
        4 * SEQ * model * hidden,
        2 * SEQ * hidden,
    )


def mlp_grad_kernel(g_ref, s_ref, w_ref, *refs):
    *before, part_ref, pre_ref, sum_ref = refs
    hidden = s_ref.shape[1]
    for span in chunks(hidden):
        shifted = slice(hidden + span.start, hidden + span.stop)
        pre = dot(g_ref[...], w_ref[:, shifted], 1, 0) * s_ref[:, span].astype(f32)
        pre = pre.astype(bf16)
        pre_ref[:, span] = pre
        add_sum([*before, sum_ref], span, pre)
    pre = pre_ref[...]
    for span in chunks(part_ref.shape[1]):
        part_ref[:, span] = dot(pre, w_ref[span, :hidden], 1, 1).astype(bf16)


def mlp_grad_image(grad, slope, weight, before):
    model, hidden = weight.shape[0], slope.shape[1]
    return run(
        mlp_grad_kernel,
        [grad, slope, weight, *before],
        [((SEQ, model), bf16), ((SEQ, hidden), bf16), ((8, hidden), f32)],
        4 * SEQ * model * hidden,
    )


def pack_images(refs, ref):
    whole, count, width = SEQ - 1, len(refs), refs[0].shape[1]
    for n, r in enumerate(refs):
        ref[n * whole : (n + 1) * whole, :width] = r[:whole, :]
    last = [r[whole:SEQ, :] for r in refs]
    last.append(jnp.zeros((ref.shape[0] - count * SEQ, width), ref.dtype))
    ref[count * whole :, :width] = jnp.concatenate(last, axis=0)


def weight_grad_kernel(rows, pairs, spot_ref, *refs):
    count = IMG_CAP
    ins, rest = refs[: 2 * count * pairs], refs[2 * count * pairs :]
    mine_ref, send_ref, left_ref, right_ref, total_ref = rest
    core = spot_ref[0, 0]
    tile = total_ref.shape[0]
    half = 2 * tile // (2 * rows)
    for pair in range(pairs):
        lefts = ins[2 * count * pair : 2 * count * pair + count]
        rights = ins[2 * count * pair + count : 2 * count * (pair + 1)]
        width = rights[0].shape[1]
        pack_images(lefts, left_ref)
        pack_images(rights, right_ref)
        at = mine_ref.shape[1] - width if pair == 0 else 0
        span = slice(at, at + width)
        for part in range(2):
            total_ref[:, :width] = dot(
                left_ref[:, part * tile : (part + 1) * tile], right_ref[:, :width], 0, 0
            )
            for z in range(rows // 2):
                to = (part * (rows // 2) + z) * half
                first = pl.multiple_of((2 * z + core) * half, 8)
                other = pl.multiple_of((2 * z + 1 - core) * half, 8)
                mine_ref[to : to + half, span] = total_ref[pl.ds(first, half), :width].astype(bf16)
                send_ref[to : to + half, span] = total_ref[pl.ds(other, half), :width].astype(bf16)


def weight_grad(pairs, spot):
    rows = lax.axis_size(ROWS)
    model = pairs[0][0][0].shape[1]
    widths = [rights[0].shape[1] for _, rights in pairs]
    wide = widths[0] if len(pairs) == 1 else tile_start(widths[1]) + widths[0]
    tokens = -(-IMG_CAP * SEQ // 16) * 16
    arrays, flops = [spot], 0
    for lefts, rights in pairs:
        arrays += [*lefts, *rights]
        flops += 2 * tokens * model * rights[0].shape[1]
    shape = (model // 2, wide)
    return run(
        functools.partial(weight_grad_kernel, rows, len(pairs)),
        arrays,
        [(shape, bf16), (shape, bf16)],
        flops,
        0,
        [
            pltpu.VMEM((tokens, model), bf16),
            pltpu.VMEM((tokens, max(widths)), bf16),
            pltpu.VMEM((model // 2, max(widths)), f32),
        ],
        20,
    )


def merge_kernel(mine_ref, got_ref, out_ref):
    out_ref[...] = (mine_ref[...].astype(f32) + got_ref[...].astype(f32)).astype(bf16)


def reduce_rows(pair):
    mine, send = pair
    got = other_core(send)
    (both,) = run(merge_kernel, [mine, got], [(mine.shape, bf16)], mine.size)
    return lax.psum_scatter(both, ROWS, scatter_dimension=0, tiled=True)


def halves(spot_ref, first_ref, second_ref, got_ref):
    mine = jnp.where(spot_ref[0, 0] == 0, first_ref[...], second_ref[...]).astype(f32)
    got = got_ref[...].astype(f32)
    here = spot_ref[0, 0] == 0
    return jnp.where(here, mine, got), jnp.where(here, got, mine)


def mlp_block_kernel(spot_ref, *refs):
    up_ref, down_ref = refs[6:]
    low, high = halves(spot_ref, *refs[:3])
    half = low.shape[0]
    up_ref[:half, :] = low
    up_ref[half:, :] = high
    low, high = halves(spot_ref, *refs[3:6])
    down_ref[...] = jnp.concatenate([low, high], axis=0).T


def attention_block_kernel(spot_ref, first_ref, second_ref, got_ref, out_ref, qkv_ref):
    low, high = halves(spot_ref, first_ref, second_ref, got_ref)
    half = low.shape[0]
    width = out_ref.shape[0]
    qkv_ref[:half, :] = low[:, width:]
    qkv_ref[half:, :] = high[:, width:]
    out_ref[...] = jnp.concatenate([low[:, :width], high[:, :width]], axis=0).T


def standardize(values):
    centre = jnp.mean(values, axis=1, keepdims=True)
    centred = values - centre
    inverse = lax.rsqrt(jnp.mean(centred * centred, axis=1, keepdims=True) + EPSILON)
    return centred * inverse, inverse


def three(a_ref, b_ref, c_ref):
    return a_ref[...].astype(f32) + b_ref[...].astype(f32) + c_ref[...].astype(f32)


def middle_kernel(layer, a_ref, b_ref, c_ref, token_ref, x_ref, vector_ref, resid_ref, out_ref):
    resid = x_ref[...].astype(f32) + (three(a_ref, b_ref, c_ref) + row(vector_ref, layer, OUT_BIAS))
    resid_ref[...] = resid
    standard, _ = standardize(resid)
    out_ref[...] = (
        standard * row(vector_ref, layer, GAIN2) + row(vector_ref, layer, SHIFT2)
    ).astype(bf16)


def layer_end(layer, spot_ref, a_ref, b_ref, c_ref, resid_ref, vector_ref):
    value = resid_ref[...] + (three(a_ref, b_ref, c_ref) + row(vector_ref, layer, DOWN_BIAS))
    return jnp.where(spot_ref[0, 2] > 0, value, jnp.zeros_like(value)).astype(bf16)


def last_kernel(
    spot_ref, a_ref, b_ref, c_ref, token_ref, resid_ref, vector_ref, x_ref, out_ref
):
    value = layer_end(0, spot_ref, a_ref, b_ref, c_ref, resid_ref, vector_ref)
    x_ref[...] = value
    standard, _ = standardize(value.astype(f32))
    out_ref[...] = (standard * row(vector_ref, 1, GAIN1) + row(vector_ref, 1, SHIFT1)).astype(bf16)


def final_kernel(spot_ref, a_ref, b_ref, c_ref, token_ref, resid_ref, vector_ref, x_ref):
    x_ref[...] = layer_end(1, spot_ref, a_ref, b_ref, c_ref, resid_ref, vector_ref)


def norm_back(grad_out, values, gain):
    standard, inverse = standardize(values)
    scaled = grad_out * gain
    mean_one = jnp.mean(scaled, axis=1, keepdims=True)
    mean_two = jnp.mean(scaled * standard, axis=1, keepdims=True)
    grad = inverse * (scaled - mean_one - standard * mean_two)
    return (
        grad,
        jnp.sum(grad_out * standard, axis=0, keepdims=True),
        jnp.sum(grad_out, axis=0, keepdims=True),
    )


def middle_grad_kernel(
    layer, a_ref, b_ref, c_ref, resid_ref, up_ref, vector_ref, grad_ref, low_ref, sum_ref
):
    upstream = up_ref[...].astype(f32)
    grad, gain_sum, shift_sum = norm_back(
        three(a_ref, b_ref, c_ref), resid_ref[...], row(vector_ref, layer, GAIN2)
    )
    grad = grad + upstream
    low = grad.astype(bf16)
    grad_ref[...] = grad
    low_ref[...] = low
    sum_ref[OUT_BIAS : OUT_BIAS + 1, :] = jnp.sum(low.astype(f32), axis=0, keepdims=True)
    sum_ref[GAIN2 : GAIN2 + 1, :] = gain_sum
    sum_ref[SHIFT2 : SHIFT2 + 1, :] = shift_sum
    sum_ref[DOWN_BIAS : DOWN_BIAS + 1, :] = jnp.sum(upstream, axis=0, keepdims=True)


def last_grad_kernel(
    layer, a_ref, b_ref, c_ref, x_ref, grad_ref, vector_ref, old_ref, out_ref, sum_ref
):
    grad, gain_sum, shift_sum = norm_back(
        three(a_ref, b_ref, c_ref), x_ref[...].astype(f32), row(vector_ref, layer, GAIN1)
    )
    out_ref[...] = (grad + grad_ref[...]).astype(bf16)
    sum_ref[OUT_BIAS:, :] = old_ref[OUT_BIAS:, :]
    sum_ref[GAIN1 : GAIN1 + 1, :] = gain_sum
    sum_ref[SHIFT1 : SHIFT1 + 1, :] = shift_sum


def sum_over(value, axis):
    bits, count = 1, lax.axis_size(axis)
    while bits < count:
        value = value + lax.ppermute(value, axis, [(k, k ^ bits) for k in range(count)])
        bits *= 2
    return value


ORDER = (0, 1, 2, 3)


def body(
    images,
    cotangent,
    live_images,
    attn_norm_gain,
    attn_norm_bias,
    qkv_weight,
    query_value_bias,
    out_weight,
    out_bias,
    mlp_norm_gain,
    mlp_norm_bias,
    up_weight,
    up_bias,
    down_weight,
    down_bias,
):
    section = lax.axis_index(CORE)
    me = lax.axis_index(COLS)
    first = section == 0
    width = images.shape[1]
    model = lax.axis_size(COLS) * width
    part, hidden = qkv_weight.shape[1], up_weight.shape[2]
    live = me < lax.dynamic_index_in_dim(live_images[0], section, 0, keepdims=False)
    spot = jnp.stack([section, me, live.astype(jnp.int32), lax.axis_index(ROWS)])
    spot = spot.astype(jnp.int32).reshape(1, 4)

    def both_layers(block):
        half = block.shape[0] // 2
        low, high = block[:half], block[half:]
        keep = jnp.where(first, low, high)
        got = other_core(jnp.where(first, high, low))
        return jnp.where(first, keep, got), jnp.where(first, got, keep)

    def gather(block):
        return lax.all_gather(block, (ROWS, CORE), axis=0, tiled=True)

    blocks = (
        jnp.concatenate(
            [
                out_weight[0].T,
                qkv_weight[0].reshape(part, 3 * width),
            ],
            axis=1,
        ),
        jnp.concatenate([up_weight[0], down_weight[0].T], axis=1),
    )
    attn_halves, mlp_halves = (both_layers(block) for block in blocks)
    weights = [
        (line_gather(attn_halves[0], spot), gather(mlp_halves[0])),
        (gather(attn_halves[1]), gather(mlp_halves[1])),
    ]

    small = jnp.concatenate(
        [
            attn_norm_gain,
            attn_norm_bias,
            out_bias,
            mlp_norm_gain,
            mlp_norm_bias,
            down_bias,
            query_value_bias[0],
            up_bias.reshape(hidden // width, width),
        ],
        axis=0,
    )
    other = other_core(small)
    small = jnp.concatenate(
        [jnp.where(first, small, other), jnp.where(first, other, small)], axis=0
    )
    local = small.astype(f32)
    small = [s.astype(f32) for s in hops([small] * IMG_CAP)]

    def pick(array):
        return hops(run(pick_kernel, [spot, array], [((SEQ, width), bf16)] * IMG_CAP, 1))

    shape = (SEQ, model)
    size = 10 * SEQ * model
    x, vector, normed = run(
        join_kernel,
        [spot, *pick(images), *small],
        [(shape, bf16), ((2 * FEATURES, model), f32), (shape, bf16)],
        size,
    )
    target = pick(cotangent)
    (target,) = run(join_target_kernel, [spot, *target], [(shape, bf16)], size)

    kept, xs = [], []
    for layer in range(2):
        attn_w, mlp_w = weights[layer]
        stage = ATTN + str(layer)
        done = {}
        wide1 = spread(normed)
        for slot in ORDER:
            done[slot] = attention_image(layer, wide1[slot], attn_w, local)
        terms, qkvs, mixed, lses = ([done[slot][n] for slot in range(4)] for n in range(4))
        terms = fold(terms, stage)
        resid, normed = run(
            functools.partial(middle_kernel, layer),
            [*terms, x, vector],
            [(shape, f32), (shape, bf16)],
            size,
        )
        stage = MLP + str(layer)
        done = {}
        wide2 = spread(normed)
        if layer == 0:
            target_wide = spread(target)
        for slot in ORDER:
            done[slot] = mlp_image(layer, wide2[slot], mlp_w, local)
        terms, active, slopes = ([done[slot][n] for slot in range(4)] for n in range(3))
        kept.append((x, resid, wide1, qkvs, mixed, lses, wide2, active, slopes))
        terms = fold(terms, stage)
        ends = [spot, *terms, resid, vector]
        if layer == 0:
            x, normed = run(last_kernel, ends, [(shape, bf16), (shape, bf16)], size)
        else:
            (x,) = run(final_kernel, ends, [(shape, bf16)], size)
        xs.append(x)

    upstream, down_wide = target, target_wide
    grads_in, mats, tokens, heads = [None] * 2, [None] * 2, [None] * 2, [None] * 2
    for layer in (1, 0):
        x, resid, wide1, qkvs, mixed, lses, wide2, active, slopes = kept[layer]
        attn_w, mlp_w = weights[layer]
        tag = str(layer)
        stage = MLP_GRAD + tag
        done, before = {}, []
        for slot in ORDER:
            done[slot] = mlp_grad_image(down_wide[slot], slopes[slot], mlp_w, before)
            before = [done[slot][2]]
        terms, pres = ([done[slot][n] for slot in range(4)] for n in range(2))
        up_sums = before[0][:1]
        up_half = weight_grad([(wide2, pres)], spot)
        down_half = weight_grad([(down_wide, active)], spot)
        terms = fold(terms, stage)
        grad_resid, grad_attn, sums = run(
            functools.partial(middle_grad_kernel, layer),
            [*terms, resid, upstream, vector],
            [(shape, f32), (shape, bf16), ((FEATURES, model), f32)],
            size,
        )
        stage = ATTN_GRAD + tag
        done, before = {}, []
        attn_wide = spread(grad_attn)
        for slot in ORDER:
            done[slot] = attention_grad_image(
                attn_wide[slot], qkvs[slot], lses[slot], attn_w, before
            )
            before = [done[slot][2]]
        terms, dqkvs = ([done[slot][n] for slot in range(4)] for n in range(2))
        heads[layer] = jnp.concatenate([before[0][:1, -3 * width :], up_sums], axis=1)
        attn_half = weight_grad([(wide1, dqkvs), (attn_wide, mixed)], spot)
        terms = fold(terms, stage)
        upstream, tokens[layer] = run(
            functools.partial(last_grad_kernel, layer),
            [*terms, x, grad_resid, vector, sums],
            [(shape, bf16), ((FEATURES, model), f32)],
            size,
        )
        grads_in[layer] = upstream
        if layer:
            down_wide = spread(upstream)
        mats[layer] = (reduce_rows(down_half), reduce_rows(up_half), reduce_rows(attn_half))

    def outputs(pair):
        got = other_core(jnp.where(first, pair[1], pair[0]))
        mine = jnp.where(first, pair[0], pair[1])
        parts = run(
            split_kernel, [spot, mine, got], [((2, SEQ, width), bf16)] * IMG_CAP, 1
        )
        parts = hops(parts)
        (whole,) = run(
            place_kernel, [spot, *parts], [((2 * IMG_CAP * SEQ, width), bf16)], 1
        )
        return whole[None]

    section_outputs = outputs(xs)
    input_grads = outputs(grads_in)

    def swapped(n):
        low, high = mats[0][n], mats[1][n]
        return [low, high, other_core(jnp.where(first, high, low))]

    grad_up, grad_down = run(
        mlp_block_kernel,
        [spot, *swapped(1), *swapped(0)],
        [((part, hidden), f32), ((hidden, part), f32)],
        size,
    )
    grad_out, grad_qkv = run(
        attention_block_kernel,
        [spot, *swapped(2)],
        [((width, part), f32), ((part, 3 * width), f32)],
        size,
    )

    by_token = sum_over(jnp.stack(tokens), COLS)
    by_token = lax.dynamic_slice_in_dim(by_token, me * width, width, 2)
    packed = jnp.concatenate(
        [by_token.reshape(2, FEATURES * width), jnp.concatenate(heads, axis=0)], axis=1
    )
    packed = sum_over(sum_over(packed, ROWS), CORE)
    packed = lax.dynamic_index_in_dim(packed, section, 0, keepdims=True)
    cut = [packed[:, n * width : (n + 1) * width] for n in range(FEATURES + 3)]
    return (
        section_outputs,
        input_grads,
        cut[GAIN1],
        cut[SHIFT1],
        grad_qkv.reshape(1, part, 3, width),
        jnp.stack([cut[FEATURES], cut[FEATURES + 2]], axis=1),
        grad_out[None],
        cut[OUT_BIAS],
        cut[GAIN2],
        cut[SHIFT2],
        grad_up[None],
        packed[:, (FEATURES + 3) * width :],
        grad_down[None],
        cut[DOWN_BIAS],
    )


def solution(mesh):
    in_specs = (
        P(ROWS, COLS),
        P(ROWS, COLS),
        P(ROWS, None),
        P(CORE, COLS),
        P(CORE, COLS),
        P(CORE, ROWS, None, COLS),
        P(CORE, None, COLS),
        P(CORE, COLS, ROWS),
        P(CORE, COLS),
        P(CORE, COLS),
        P(CORE, COLS),
        P(CORE, ROWS, COLS),
        P(CORE, COLS),
        P(CORE, COLS, ROWS),
        P(CORE, COLS),
    )
    out_specs = (
        P(CORE, ROWS, COLS),
        P(CORE, ROWS, COLS),
        P(CORE, COLS),
        P(CORE, COLS),
        P(CORE, ROWS, None, COLS),
        P(CORE, None, COLS),
        P(CORE, COLS, ROWS),
        P(CORE, COLS),
        P(CORE, COLS),
        P(CORE, COLS),
        P(CORE, ROWS, COLS),
        P(CORE, COLS),
        P(CORE, COLS, ROWS),
        P(CORE, COLS),
    )

    return jax.shard_map(body, mesh=mesh, in_specs=in_specs, out_specs=out_specs, check_vma=False)
```
